32 devices in a mesh: node: 8 (over y, x, core), harm: 4 (over z).
Axes of the slice: x: 2, y: 2, z: 4, core: 2. Of those that a mesh axis runs over, the one named last changes fastest.
Arguments:
- krylov_basis: float32 [8, 2, 64, 16384], P(None, None, 'harm', 'node'), may hold values from -100 to 100, as said below
- cond_time: float32 [64, 16384], P('harm', 'node'), may hold values from 2 to 6
- capacity: float32 [16384], P('node'), may hold values from 0.005 to 0.05
- diag_blocks: float32 [64, 256, 256], P('node'), may hold values from -1 to 1
- coupling: float32 [64, 2, 256, 256], P('node'), may hold values from -0.375 to 0.375
- neighbours: int32 [64, 2], P('node'), may hold values from 0 to 63, as said below
- pattern: int32 [64, 2], P('node'), may hold values from 0 to 1
Outputs:
- new_vector: float32 [2, 64, 16384], P(None, 'harm', 'node')
- projections: float32 [2, 8], replicated
- new_norm: float32 [], replicated
The draws below stay inside these ranges and needn't reach their ends.
Inputs may be any that keep to these rules, and one draw needn't show every extreme that they name: `neighbours`: with the blocks in groups of 8 consecutive ones, each entry lies in a group 1 to 3 groups away from its row's group; the present slots of the rows of one group name at most 2 distinct blocks of any other group. `krylov_basis`: each of the 8 vectors has mean squared entry 1 over its real and imaginary parts.
All inputs are finite; a program needn't handle non-finite values.
Results may differ from the reference program's by a relative error of at most 0.0003.
Values sent between devices are 32-bit elements; how exact they have to be, the bound alone decides.
A program may use at most 64 MiB of HBM per device.

```python
import math
import jax
import jax.numpy as jnp
from jax import lax

BS = 256
H = 64
BLK_DEV = 8
NEIGH = 2
KRY = 8
NS_ITERS = 4
USED = 2
BLOCKS = 64
NODES = 16384


def draw_krylov_basis(key, part):
    keys = jax.random.split(jax.random.fold_in(key, 11), 4)
    fresh = jax.random.truncated_normal(keys[0], -4.0, 4.0, (KRY, 2, H, BLOCKS * BS), jnp.float32)
    common = jax.random.truncated_normal(keys[1], -4.0, 4.0, (1, 2, H, BLOCKS * BS), jnp.float32)
    harmonic_scale = jnp.exp(jax.random.uniform(keys[2], (H,), jnp.float32, 0.0, math.log(10.0)))
    block_scale = jnp.exp(jax.random.uniform(keys[3], (BLOCKS,), jnp.float32, 0.0, math.log(10.0)))
    field = harmonic_scale[:, None] * jnp.repeat(block_scale, BS)[None, :]
    mixed = 0.85 * fresh + 0.5 * common
    vectors = field[None, None] * mixed
    spread = jnp.sqrt(jnp.mean(vectors * vectors, axis=(1, 2, 3), keepdims=True))
    return (vectors / spread).astype(jnp.float32)


def coupling_layout(key):
    keys = jax.random.split(jax.random.fold_in(key, 23), 5)
    groups = BLOCKS // BLK_DEV
    slots = BLK_DEV * NEIGH
    hot_keys = jax.random.split(keys[0], groups * 6)
    hot = jax.vmap(lambda k: jax.random.permutation(k, BLK_DEV))(hot_keys)[:, :USED]
    hot = hot.reshape(groups, 6, USED).astype(jnp.int32)
    slot_ids = jnp.arange(slots, dtype=jnp.int32)
    forced = jnp.broadcast_to(slot_ids < 6 * USED, (groups, slots))
    random_side = jax.random.randint(keys[1], (groups, slots), 0, 6, dtype=jnp.int32)
    random_pick = jax.random.randint(keys[2], (groups, slots), 0, USED, dtype=jnp.int32)
    side = jnp.where(forced, (slot_ids // USED)[None, :], random_side)
    pick = jnp.where(forced, (slot_ids % USED)[None, :], random_pick)
    order = jax.vmap(lambda k: jax.random.permutation(k, slots))(jax.random.split(keys[3], groups)).astype(jnp.int32)
    side = jnp.take_along_axis(side, order, axis=1)
    pick = jnp.take_along_axis(pick, order, axis=1)
    forced = jnp.take_along_axis(forced, order, axis=1)
    table = jnp.array([1, 2, 3, -1, -2, -3], dtype=jnp.int32)
    offsets = table[side]
    group = jnp.arange(groups, dtype=jnp.int32)[:, None]
    target = group + offsets
    flip = (target < 0) | (target >= groups)
    side = jnp.where(flip, (side + 3) % 6, side)
    target = jnp.where(flip, group - offsets, target)
    chosen = hot[group, side, pick]
    neighbours = (target * BLK_DEV + chosen).reshape(BLOCKS, NEIGH).astype(jnp.int32)
    present = (jax.random.randint(keys[4], (groups, slots), 0, 4, dtype=jnp.int32) > 0) | forced
    pattern = present.astype(jnp.int32).reshape(BLOCKS, NEIGH)
    return (neighbours, pattern)


def draw_neighbours(key, part):
    return coupling_layout(key)[0]


def draw_pattern(key, part):
    return coupling_layout(key)[1]


def level_of(own_key, extent, cuts, least, high):
    loudness = 1.0
    for axis_at, parts in cuts:
        draws = jax.random.uniform(jax.random.fold_in(jax.random.fold_in(own_key, 6), axis_at), (parts,), jnp.float32, least / len(cuts), high / len(cuts))
        loudness = loudness * jnp.repeat(jnp.exp(draws), extent[axis_at] // parts).reshape((-1,) + (1,) * (len(extent) - 1 - axis_at))
    return loudness


def scatter_about(rng, extent, scale, limit, shards=(), kind=jnp.bfloat16):
    drawn = jax.random.normal(rng, extent, jnp.float32) * scale
    if len(shards) > 0:
        drawn = level_of(rng, extent, shards, -0.22, 0.18) * drawn
    return jnp.clip(drawn, min=-limit, max=limit).astype(kind)


def setup_inputs(seed: int = 0) -> dict:
    key_list = jax.random.split(jax.random.key(seed), 8)
    return {
        "krylov_basis": draw_krylov_basis(jax.random.fold_in(key_list[7], 71), 0),
        "cond_time": jnp.clip(jnp.exp(math.log(6.0) - 1.0986123 * jax.random.uniform(key_list[1], (H, NODES), jnp.float32) ** level_of(key_list[1], (H, NODES), ((0, 4), (1, 8)), -0.2, 0.2)), 2.0, 6.0),
        "capacity": jnp.clip(jnp.exp(math.log(0.05) - 2.3025851 * jax.random.uniform(key_list[2], (NODES,), jnp.float32) ** level_of(key_list[2], (NODES,), ((0, 8),), -0.2, 0.2)), 0.005, 0.05),
        "diag_blocks": scatter_about(key_list[3], (BLOCKS, BS, BS), (BS // 8 + 2) ** -0.5, 1.0, ((0, 8),), jnp.float32),
        "coupling": scatter_about(key_list[4], (BLOCKS, NEIGH, BS, BS), BS ** -0.5, 0.375, ((0, 8),), jnp.float32),
        "neighbours": draw_neighbours(jax.random.fold_in(key_list[7], 71), 0),
        "pattern": draw_pattern(jax.random.fold_in(key_list[7], 71), 0),
    }


precise = lax.Precision.HIGHEST

def spectral_table(count):
    steps = jnp.arange(count, dtype=jnp.int32)
    phases = steps[:, None] * steps[None, :] % count
    angles = phases.astype(jnp.float32) * (2.0 * math.pi / count)
    factor = 1.0 / math.sqrt(count)
    cosine = jnp.cos(angles) * factor
    sine = jnp.sin(angles) * factor
    upper = jnp.concatenate([cosine, -sine], axis=1)
    lower = jnp.concatenate([sine, cosine], axis=1)
    return jnp.concatenate([upper, lower], axis=0)

def newton_inverse(blocks, means):
    width = blocks.shape[-1]
    identity = jnp.eye(width, dtype=jnp.float32)
    matrix = blocks + identity * means[:, None, :]
    inverse = identity * (1.0 / means)[:, None, :]
    for iteration in range(NS_ITERS):
        product = jnp.einsum('bij,bjk->bik', matrix, inverse, precision=precise)
        inverse = jnp.einsum('bij,bjk->bik', inverse, 2.0 * identity - product, precision=precise)
    return inverse

def reference(krylov_basis, cond_time, capacity, diag_blocks, coupling, neighbours, pattern):
    means = lax.optimization_barrier(jnp.sum(cond_time, axis=0)) / H
    inverse = newton_inverse(diag_blocks, means.reshape(BLOCKS, BS))
    vector = krylov_basis[KRY - 1].reshape(2, H, BLOCKS, BS)
    solved = jnp.einsum('bmn,phbn->phbm', inverse, vector, precision=precise)
    picked = jnp.take(solved, neighbours.reshape(-1).astype(jnp.int32), axis=2)
    picked = picked.reshape(2, H, BLOCKS, NEIGH, BS) * pattern.astype(jnp.float32)[None, None, :, :, None]
    coupled = jnp.einsum('bjmn,phbjn->phbm', coupling, picked, precision=precise).reshape(2, H, NODES)
    direct = jnp.einsum('bmn,phbn->phbm', diag_blocks, solved, precision=precise).reshape(2, H, NODES)
    table = spectral_table(H)
    samples = jnp.dot(table, solved.reshape(2 * H, NODES), precision=precise).reshape(2, H, NODES)
    driven = (samples * cond_time[None]).reshape(2 * H, NODES)
    spectra = jnp.dot(table.T, driven, precision=precise).reshape(2, H, NODES)
    solved_flat = solved.reshape(2, H, NODES)
    harmonics = jnp.arange(H, dtype=jnp.int32)
    omega = ((harmonics + H // 2) % H - H // 2).astype(jnp.float32)
    react = omega[:, None] * capacity[None, :]
    image_real = direct[0] + spectra[0] + coupled[0] - react * solved_flat[1]
    image_imag = direct[1] + spectra[1] + coupled[1] + react * solved_flat[0]
    count = H * NODES
    basis_real = krylov_basis[:, 0].reshape(KRY, -1)
    basis_imag = krylov_basis[:, 1].reshape(KRY, -1)
    flat_real = image_real.reshape(-1)
    flat_imag = image_imag.reshape(-1)
    proj_real = (jnp.dot(basis_real, flat_real, precision=precise) + jnp.dot(basis_imag, flat_imag, precision=precise)) / count
    proj_imag = (jnp.dot(basis_real, flat_imag, precision=precise) - jnp.dot(basis_imag, flat_real, precision=precise)) / count
    rest_real = flat_real - (jnp.dot(proj_real, basis_real, precision=precise) - jnp.dot(proj_imag, basis_imag, precision=precise))
    rest_imag = flat_imag - (jnp.dot(proj_real, basis_imag, precision=precise) + jnp.dot(proj_imag, basis_real, precision=precise))
    squares = (jnp.sum(rest_real * rest_real) + jnp.sum(rest_imag * rest_imag)) / count
    new_norm = jnp.sqrt(squares + 1e-06)
    new_vector = jnp.stack([rest_real, rest_imag]).reshape(2, H, NODES) / new_norm
    return (new_vector, jnp.stack([proj_real, proj_imag]), new_norm)
```

```python
import functools
import math

import jax
import jax.numpy as jnp
import numpy as np
from jax import lax
from jax.experimental import pallas as pl
from jax.experimental.pallas import tpu as pltpu
from jax.sharding import PartitionSpec as P

NS_ITERS = 4
REACH = 3
USED = 2
OFFSETS = tuple(o for o in range(-REACH, REACH + 1) if o != 0)
MESH = pl.DeviceIdType.MESH
NN = (((1,), (0,)), ((), ()))
NT = (((1,), (1,)), ((), ()))


def split(x):
    high = x.astype(jnp.bfloat16)
    low = (x - high.astype(jnp.float32)).astype(jnp.bfloat16)
    return high, low


def mm(x, weights, dims):
    xh, xl = x
    wh, wl = weights
    rows = xh.shape[0]
    dot = functools.partial(
        lax.dot_general, dimension_numbers=dims, preferred_element_type=jnp.float32
    )
    both = dot(jnp.concatenate([xh, xl], axis=0), wh)
    return both[:rows] + (both[rows:] + dot(xh, wl))


def spectral_tables(count, parts):
    steps = np.arange(count)
    angles = (steps[:, None] * steps[None, :] % count) * (2.0 * math.pi / count)
    cosine = np.cos(angles) / math.sqrt(count)
    sine = np.sin(angles) / math.sqrt(count)
    table = np.block([[cosine, -sine], [sine, cosine]])
    own = count // parts
    ordered = table.reshape(2 * count, 2, parts, own).transpose(0, 2, 1, 3).reshape(2 * count, -1)
    tables = np.stack([ordered, ordered.T]).astype(np.float32)
    high = tables.astype(jnp.bfloat16)
    low = (tables - high.astype(np.float32)).astype(jnp.bfloat16)
    return np.stack([high, low], axis=1)


def kernel(
    nodes, harms,
    where_ref, request_ref, tables_ref, capacity_ref, basis_hbm, cond_hbm, diag_hbm, coupling_hbm,
    new_ref, proj_ref, norm_ref,
    basis, cond, diag, coupling, sums, wanted, cond_cols, esplit, e2split, e4split,
    solved, columns, packed, received, spectra_cols, spectra, image,
    part_node, part_harm, square_node, square_harm,
    load_sem, send_sem, recv_sem,
):
    node = lax.axis_index("node")
    harm = lax.axis_index("harm")
    kry, _, own, width = basis.shape
    blocks, bs, _ = diag.shape
    rows = 2 * own
    period = own * harms
    piece = width // harms
    last = kry - 1

    loads = [
        pltpu.make_async_copy(cond_hbm, cond, load_sem.at[0]),
        pltpu.make_async_copy(diag_hbm, diag, load_sem.at[1]),
        pltpu.make_async_copy(basis_hbm, basis, load_sem.at[2]),
        pltpu.make_async_copy(coupling_hbm, coupling, load_sem.at[3]),
    ]
    for load in loads:
        load.start()

    barrier = pltpu.get_barrier_semaphore()
    for step in range(1, harms):
        pl.semaphore_signal(
            barrier, inc=1, device_id={"harm": lax.rem(harm + step, harms)}, device_id_type=MESH
        )
    for step in range(1, nodes):
        pl.semaphore_signal(
            barrier, inc=1, device_id={"node": lax.rem(node + step, nodes)}, device_id_type=MESH
        )
    pl.semaphore_wait(barrier, harms - 1 + nodes - 1)

    counter = [0]

    def reserve(count):
        first = counter[0]
        counter[0] += count
        return first

    def around(axis, count, source, target):
        me = harm if axis == "harm" else node
        first = reserve(count)
        copies = []
        for step in range(1, count):
            peer = lax.rem(me + step, count)
            copies.append(
                pltpu.make_async_remote_copy(
                    src_ref=source(peer),
                    dst_ref=target,
                    send_sem=send_sem.at[first + step],
                    recv_sem=recv_sem.at[first + step],
                    device_id={axis: peer},
                    device_id_type=MESH,
                )
            )
            copies[-1].start()
        return copies

    def finish(copies):
        for copy in copies:
            copy.wait()

    def neighbour_copies(source, target):
        first = reserve(len(OFFSETS))
        out = []
        for at, offset in enumerate(OFFSETS):
            peer = node + offset
            copy = pltpu.make_async_remote_copy(
                src_ref=source.at[at],
                dst_ref=target.at[len(OFFSETS) - 1 - at],
                send_sem=send_sem.at[first + at],
                recv_sem=recv_sem.at[first + at],
                device_id={"node": jnp.clip(peer, 0, nodes - 1)},
                device_id_type=MESH,
            )
            sends = jnp.logical_and(peer >= 0, peer < nodes)
            back = node - offset
            receives = jnp.logical_and(back >= 0, back < nodes)
            pl.when(sends)(copy.start)
            out.append((copy, sends, receives))
        return out

    def neighbour_finish(copies):
        for copy, sends, receives in copies:
            pl.when(sends)(copy.wait_send)
            pl.when(receives)(copy.wait_recv)

    loads[0].wait()
    sums[harm] = jnp.sum(cond[...], axis=0, keepdims=True)
    sum_copies = around("harm", harms, lambda peer: sums.at[harm], sums.at[harm])
    request_copies = neighbour_copies(request_ref, wanted)
    cond_copies = around(
        "harm", harms,
        lambda peer: cond.at[:, pl.ds(pl.multiple_of(peer * piece, 128), piece)],
        cond_cols.at[harm],
    )
    mine = pl.ds(pl.multiple_of(harm * piece, 128), piece)
    cond_cols[harm] = cond[:, mine]
    received[len(OFFSETS), 0] = jnp.zeros((rows, bs), jnp.float32)
    loads[1].wait()
    loads[2].wait()
    finish(sum_copies)
    total = sums[0]
    for at in range(1, harms):
        total = total + sums[at]
    means = total / period
    inverse_means = 1.0 / means
    norm_means = means

    together = 2
    sums[harm] = means

    def lanes(b):
        return pl.ds(pl.multiple_of(b * bs, 128), bs)

    def solve(i, carry):
        ids = [i * together + k for k in range(together)]
        scale = []
        for b in ids:
            local = sums[harm, :, lanes(b)]
            scale.append(1.0 / local)
        e1 = [split(-diag[b] * s) for b, s in zip(ids, scale)]
        for b, e in zip(ids, e1):
            esplit[b, 0] = e[0]
            esplit[b, 1] = e[1]
        e2 = [split(mm(e, e, NN)) for e in e1]
        e4 = [split(mm(e, e, NN)) for e in e2]
        w = [basis[last, :, :, lanes(b)].reshape(rows, bs) for b in ids]
        for power in (e1, e2, e4):
            w = [x + mm(split(x), e, NT) for x, e in zip(w, power)]
        y = [mm(split(x), e, NT) for x, e in zip(w, e4)]
        y = [mm(split(x), e, NT) for x, e in zip(y, e4)]
        for b, x, z, s in zip(ids, w, y, scale):
            solved[:, :, lanes(b)] = ((x + z) * s).reshape(2, own, bs)
        return carry

    lax.fori_loop(0, blocks // together, solve, 0)

    column_copies = around(
        "harm", harms,
        lambda peer: solved.at[:, :, pl.ds(pl.multiple_of(peer * piece, 128), piece)],
        columns.at[harm],
    )
    columns[harm] = solved[:, :, mine]
    neighbour_finish(request_copies)
    for at in range(len(OFFSETS)):
        for slot in range(USED):
            chosen = jnp.zeros((rows, bs), jnp.float32)
            for b in range(blocks):
                line = slot * blocks + b
                flag = jnp.concatenate([wanted[at, line : line + 1, :]] * (bs // 128), axis=1)
                value = solved[:, :, b * bs : (b + 1) * bs].reshape(rows, bs)
                chosen = jnp.where(flag > 0.5, value, chosen)
            packed[at, slot] = chosen
    block_copies = neighbour_copies(packed, received)

    def direct(i, carry):
        for k in range(together):
            b = i * together + k
            local = sums[harm, :, lanes(b)]
            here = solved[:, :, lanes(b)]
            weights = (esplit[b, 0], esplit[b, 1])
            out = mm(split(here.reshape(rows, bs) * local), weights, NT).reshape(2, own, bs)
            k_at = harm * own + lax.broadcasted_iota(jnp.int32, (own, bs), 0)
            omega = (lax.rem(k_at + period // 2, period) - period // 2).astype(jnp.float32)
            react = omega * capacity_ref[:, lanes(b)]
            image[0, :, lanes(b)] = -out[0] - react * here[1]
            image[1, :, lanes(b)] = -out[1] + react * here[0]
        return carry

    lax.fori_loop(0, blocks // together, direct, 0)

    finish(cond_copies)
    finish(column_copies)
    field = columns[...].reshape(2 * period, piece)
    def table_apply(which, field):
        th = tables_ref[which, 0]
        tl = tables_ref[which, 1]
        return mm((th, tl), split(field), NN)
    samples = table_apply(0, field).reshape(2, period, piece)
    driven = samples * cond_cols[...].reshape(period, piece)[None]
    spectra_cols[...] = table_apply(1, driven.reshape(2 * period, piece)).reshape(
        harms, 2, own, piece
    )
    spectra_copies = around("harm", harms, lambda peer: spectra_cols.at[peer], spectra.at[harm])
    spectra[harm] = spectra_cols[harm]

    loads[3].wait()
    neighbour_finish(block_copies)

    def couple(b, carry):
        out = image[:, :, lanes(b)].reshape(rows, bs)
        for slot in range(coupling.shape[1]):
            line = where_ref[b, slot]
            picked = received[line // USED, lax.rem(line, USED)]
            out = out + mm(split(picked), split(coupling[b, slot]), NT)
        image[:, :, lanes(b)] = out.reshape(2, own, bs)
        return carry

    lax.fori_loop(0, blocks, couple, 0, unroll=2)
    finish(spectra_copies)

    for at in range(harms):
        area = pl.ds(at * piece, piece)
        image[:, :, area] = image[:, :, area] + spectra[at]

    def fold(x):
        x = x.reshape(own // 8, 8, x.shape[1]).sum(0)
        out = x[:, 0:128]
        for at in range(1, x.shape[1] // 128):
            out = out + x[:, at * 128 : (at + 1) * 128]
        return jnp.sum(out, axis=0, keepdims=True)

    def exchange(parts_node, parts_harm):
        finish(around("node", nodes, lambda peer: parts_node.at[node], parts_node.at[node]))
        value = parts_node[0]
        for at in range(1, nodes):
            value = value + parts_node[at]
        parts_harm[harm] = value
        finish(around("harm", harms, lambda peer: parts_harm.at[harm], parts_harm.at[harm]))
        value = parts_harm[0]
        for at in range(1, harms):
            value = value + parts_harm[at]
        return jnp.sum(value, axis=1, keepdims=True)

    count = float(period * width * nodes)
    for m in range(kry):
        br, bi = basis[m, 0], basis[m, 1]
        part_node[node, m : m + 1] = fold(br * image[0] + bi * image[1])
        part_node[node, kry + m : kry + m + 1] = fold(br * image[1] - bi * image[0])
    proj = exchange(part_node, part_harm) / count
    proj_ref[...] = jnp.broadcast_to(proj, proj_ref.shape)

    squares = jnp.zeros((1, 128), jnp.float32)
    tile = 512
    for at in range(0, width, tile):
        area = slice(at, at + tile)
        real, imag = image[0, :, area], image[1, :, area]
        for m in range(kry):
            pr = jnp.broadcast_to(proj[m : m + 1], (own, tile))
            pi = jnp.broadcast_to(proj[kry + m : kry + m + 1], (own, tile))
            br, bi = basis[m, 0, :, area], basis[m, 1, :, area]
            real = real - (pr * br - pi * bi)
            imag = imag - (pr * bi + pi * br)
        image[0, :, area] = real
        image[1, :, area] = imag
        squares = squares + fold(real * real + imag * imag)
    square_node[node] = jnp.concatenate([squares, jnp.zeros((7, 128), jnp.float32)], axis=0)
    square = exchange(square_node, square_harm)[0:1] / count
    norm = jnp.sqrt(square + 1e-6)
    norm_ref[...] = jnp.broadcast_to(norm, norm_ref.shape)
    inverse_norm = 1.0 / norm
    for p in range(2):
        new_ref[p] = image[p] * jnp.broadcast_to(inverse_norm, (own, width))


def coupling_tables(neighbours, pattern, blocks):
    node = lax.axis_index("node")
    flat = neighbours.reshape(-1)
    present = pattern.reshape(-1) != 0
    offset = flat // blocks - node
    at = jnp.where(offset < 0, offset + REACH, offset + REACH - 1)
    block = flat % blocks
    kinds = jnp.arange(len(OFFSETS))
    numbers = jnp.arange(blocks)
    hits = (
        present[:, None, None]
        & (at[:, None, None] == kinds[None, :, None])
        & (block[:, None, None] == numbers[None, None, :])
    )
    used = jnp.any(hits, axis=0)
    before = jnp.sum(used[:, None, :] & (numbers[None, None, :] < numbers[None, :, None]), axis=2)
    slots = jnp.arange(USED)
    flags = used[:, None, :] & (before[:, None, :] == slots[None, :, None])
    request = jnp.broadcast_to(
        flags.reshape(len(OFFSETS), USED * blocks, 1).astype(jnp.float32),
        (len(OFFSETS), USED * blocks, 128),
    )
    slot = jnp.sum(jnp.where(hits, before[None], 0), axis=(1, 2))
    where = jnp.where(present, at * USED + slot, len(OFFSETS) * USED)
    where = jnp.clip(where, 0, len(OFFSETS) * USED)
    return where.reshape(neighbours.shape).astype(jnp.int32), request


def per_device(nodes, harms, krylov_basis, cond_time, capacity, diag_blocks, coupling, neighbours, pattern):
    kry, _, own, width = krylov_basis.shape
    blocks, bs, _ = diag_blocks.shape
    period = own * harms
    piece = width // harms
    rows = 2 * own
    where, request = coupling_tables(neighbours, pattern, blocks)
    tables = jnp.asarray(spectral_tables(period, harms))
    kinds = len(OFFSETS)
    sems = 5 * harms + 2 * kinds + 2 * nodes + 2 * harms
    f32, bf16 = jnp.float32, jnp.bfloat16
    vmem = pl.BlockSpec(memory_space=pltpu.VMEM)
    hbm = pl.BlockSpec(memory_space=pl.ANY)
    new, proj, norm = pl.pallas_call(
        functools.partial(kernel, nodes, harms),
        out_shape=(
            jax.ShapeDtypeStruct((2, own, width), f32),
            jax.ShapeDtypeStruct((2 * kry, 128), f32),
            jax.ShapeDtypeStruct((8, 128), f32),
        ),
        in_specs=[pl.BlockSpec(memory_space=pltpu.SMEM), vmem, vmem, vmem, hbm, hbm, hbm, hbm],
        out_specs=(vmem, vmem, vmem),
        scratch_shapes=[
            pltpu.VMEM(krylov_basis.shape, f32),
            pltpu.VMEM(cond_time.shape, f32),
            pltpu.VMEM(diag_blocks.shape, f32),
            pltpu.VMEM(coupling.shape, f32),
            pltpu.VMEM((harms, 1, width), f32),
            pltpu.VMEM((kinds, USED * blocks, 128), f32),
            pltpu.VMEM((harms, own, piece), f32),
            pltpu.VMEM((blocks, 2, bs, bs), bf16),
            pltpu.VMEM((1, 2, bs, bs), bf16),
            pltpu.VMEM((1, 2, bs, bs), bf16),
            pltpu.VMEM((2, own, width), f32),
            pltpu.VMEM((harms, 2, own, piece), f32),
            pltpu.VMEM((kinds, USED, rows, bs), f32),
            pltpu.VMEM((kinds + 1, USED, rows, bs), f32),
            pltpu.VMEM((harms, 2, own, piece), f32),
            pltpu.VMEM((harms, 2, own, piece), f32),
            pltpu.VMEM((2, own, width), f32),
            pltpu.VMEM((nodes, 2 * kry, 128), f32),
            pltpu.VMEM((harms, 2 * kry, 128), f32),
            pltpu.VMEM((nodes, 8, 128), f32),
            pltpu.VMEM((harms, 8, 128), f32),
            pltpu.SemaphoreType.DMA((4,)),
            pltpu.SemaphoreType.DMA((sems,)),
            pltpu.SemaphoreType.DMA((sems,)),
        ],
        compiler_params=pltpu.CompilerParams(
            collective_id=0, has_side_effects=True, vmem_limit_bytes=60 * 1024 * 1024
        ),
        name="arnoldi_step",
    )(where, request, tables, capacity.reshape(1, width), krylov_basis, cond_time, diag_blocks, coupling)
    return new, proj[:, 0].reshape(2, kry), norm[0, 0]


def solution(mesh):
    shape = dict(mesh.shape)
    return jax.shard_map(
        functools.partial(per_device, shape["node"], shape["harm"]),
        mesh=mesh,
        in_specs=(
            P(None, None, "harm", "node"),
            P("harm", "node"),
            P("node"),
            P("node", None, None),
            P("node", None, None, None),
            P("node", None),
            P("node", None),
        ),
        out_specs=(P(None, "harm", "node"), P(), P()),
        check_vma=False,
    )
```

```python
import functools
import math

import jax
import jax.numpy as jnp
import numpy as np
from jax import lax
from jax.experimental import pallas as pl
from jax.experimental.pallas import tpu as pltpu
from jax.sharding import PartitionSpec as P

NS_ITERS = 4
REACH = 3
USED = 2
OFFSETS = tuple(o for o in range(-REACH, REACH + 1) if o != 0)
MESH = pl.DeviceIdType.MESH
NN = (((1,), (0,)), ((), ()))
NT = (((1,), (1,)), ((), ()))


def split(x):
    high = x.astype(jnp.bfloat16)
    low = (x - high.astype(jnp.float32)).astype(jnp.bfloat16)
    return high, low


def mm(x, weights, dims):
    xh, xl = x
    wh, wl = weights
    rows = xh.shape[0]
    dot = functools.partial(
        lax.dot_general, dimension_numbers=dims, preferred_element_type=jnp.float32
    )
    both = dot(jnp.concatenate([xh, xl], axis=0), wh)
    return both[:rows] + (both[rows:] + dot(xh, wl))


def spectral_tables(count, parts):
    steps = np.arange(count)
    angles = (steps[:, None] * steps[None, :] % count) * (2.0 * math.pi / count)
    cosine = np.cos(angles) / math.sqrt(count)
    sine = np.sin(angles) / math.sqrt(count)
    table = np.block([[cosine, -sine], [sine, cosine]])
    own = count // parts
    ordered = table.reshape(2 * count, 2, parts, own).transpose(0, 2, 1, 3).reshape(2 * count, -1)
    tables = np.stack([ordered, ordered.T]).astype(np.float32)
    high = tables.astype(jnp.bfloat16)
    low = (tables - high.astype(np.float32)).astype(jnp.bfloat16)
    return np.stack([high, low], axis=1)


def kernel(
    nodes, harms,
    near_ref, pattern_ref, tables_ref, capacity_ref, basis_hbm, cond_hbm, diag_hbm, coupling_hbm,
    new_ref, proj_ref, norm_ref,
    basis, cond, diag, coupling, sums, wanted, cond_cols, esplit, where_ref, request,
    solved, columns, packed, received, spectra_cols, spectra, image,
    part_node, part_harm, square_node, square_harm,
    load_sem, send_sem, recv_sem,
):
    node = lax.axis_index("node")
    harm = lax.axis_index("harm")
    kry, _, own, width = basis.shape
    blocks, bs, _ = diag.shape
    rows = 2 * own
    period = own * harms
    piece = width // harms
    last = kry - 1

    loads = [
        pltpu.make_async_copy(cond_hbm, cond, load_sem.at[0]),
        pltpu.make_async_copy(diag_hbm, diag, load_sem.at[1]),
        pltpu.make_async_copy(basis_hbm.at[last], basis.at[last], load_sem.at[2]),
        pltpu.make_async_copy(coupling_hbm, coupling, load_sem.at[3]),
        pltpu.make_async_copy(basis_hbm.at[0:last], basis.at[0:last], load_sem.at[4]),
    ]
    for load in loads:
        load.start()

    barrier = pltpu.get_barrier_semaphore()
    for step in range(1, harms):
        pl.semaphore_signal(
            barrier, inc=1, device_id={"harm": lax.rem(harm + step, harms)}, device_id_type=MESH
        )
    for step in range(1, nodes):
        pl.semaphore_signal(
            barrier, inc=1, device_id={"node": lax.rem(node + step, nodes)}, device_id_type=MESH
        )
    coupling_tables(node, near_ref, pattern_ref, where_ref, request)
    received[len(OFFSETS), 0] = jnp.zeros((rows, bs), jnp.float32)
    loads[0].wait()
    sums[harm] = jnp.sum(cond[...], axis=0, keepdims=True)
    pl.semaphore_wait(barrier, harms - 1 + nodes - 1)

    counter = [0]

    def reserve(count):
        first = counter[0]
        counter[0] += count
        return first

    def around(axis, count, source, target):
        me = harm if axis == "harm" else node
        first = reserve(count)
        copies = []
        for step in range(1, count):
            peer = lax.rem(me + step, count)
            copies.append(
                pltpu.make_async_remote_copy(
                    src_ref=source(peer),
                    dst_ref=target,
                    send_sem=send_sem.at[first + step],
                    recv_sem=recv_sem.at[first + step],
                    device_id={axis: peer},
                    device_id_type=MESH,
                )
            )
            copies[-1].start()
        return copies

    def finish(copies):
        for copy in copies:
            copy.wait()

    def neighbour_copies(source, target):
        first = reserve(len(OFFSETS))
        out = []
        for at, offset in enumerate(OFFSETS):
            peer = node + offset
            copy = pltpu.make_async_remote_copy(
                src_ref=source.at[at],
                dst_ref=target.at[len(OFFSETS) - 1 - at],
                send_sem=send_sem.at[first + at],
                recv_sem=recv_sem.at[first + at],
                device_id={"node": jnp.clip(peer, 0, nodes - 1)},
                device_id_type=MESH,
            )
            sends = jnp.logical_and(peer >= 0, peer < nodes)
            back = node - offset
            receives = jnp.logical_and(back >= 0, back < nodes)
            pl.when(sends)(copy.start)
            out.append((copy, sends, receives))
        return out

    def neighbour_finish(copies):
        for copy, sends, receives in copies:
            pl.when(sends)(copy.wait_send)
            pl.when(receives)(copy.wait_recv)

    sum_copies = around("harm", harms, lambda peer: sums.at[harm], sums.at[harm])
    request_copies = neighbour_copies(request, wanted)
    cond_copies = around(
        "harm", harms,
        lambda peer: cond.at[:, pl.ds(pl.multiple_of(peer * piece, 128), piece)],
        cond_cols.at[harm],
    )
    mine = pl.ds(pl.multiple_of(harm * piece, 128), piece)
    cond_cols[harm] = cond[:, mine]
    loads[1].wait()
    loads[2].wait()
    finish(sum_copies)
    total = sums[0]
    for at in range(1, harms):
        total = total + sums[at]
    means = total / period

    together = 2
    sums[harm] = means

    def lanes(b):
        return pl.ds(pl.multiple_of(b * bs, 128), bs)

    def solve(ids):
        scale = [1.0 / sums[harm, :, lanes(b)] for b in ids]
        e1 = [split(-diag[b] * s) for b, s in zip(ids, scale)]
        for b, e in zip(ids, e1):
            esplit[b, 0] = e[0]
            esplit[b, 1] = e[1]
        e2 = [split(mm(e, e, NN)) for e in e1]
        e4 = [split(mm(e, e, NN)) for e in e2]
        w = [basis[last, :, :, lanes(b)].reshape(rows, bs) for b in ids]
        for power in (e1, e2, e4):
            w = [x + mm(split(x), e, NT) for x, e in zip(w, power)]
        y = [mm(split(x), e, NT) for x, e in zip(w, e4)]
        y = [mm(split(x), e, NT) for x, e in zip(y, e4)]
        for b, x, z, s in zip(ids, w, y, scale):
            solved[:, :, lanes(b)] = ((x + z) * s).reshape(2, own, bs)

    first_column = reserve(harms)
    column_copies = []
    per_piece = piece // bs
    for step in range(1, harms + 1):
        peer = lax.rem(harm + step, harms)
        solve([peer * per_piece + k for k in range(per_piece)])
        if step < harms:
            copy = pltpu.make_async_remote_copy(
                src_ref=solved.at[:, :, pl.ds(pl.multiple_of(peer * piece, 128), piece)],
                dst_ref=columns.at[harm],
                send_sem=send_sem.at[first_column + step],
                recv_sem=recv_sem.at[first_column + step],
                device_id={"harm": peer},
                device_id_type=MESH,
            )
            copy.start()
            column_copies.append(copy)
    columns[harm] = solved[:, :, mine]
    neighbour_finish(request_copies)
    for at in range(len(OFFSETS)):
        for slot in range(USED):
            chosen = jnp.zeros((rows, bs), jnp.float32)
            for b in range(blocks):
                line = slot * blocks + b
                flag = jnp.concatenate([wanted[at, line : line + 1, :]] * (bs // 128), axis=1)
                value = solved[:, :, b * bs : (b + 1) * bs].reshape(rows, bs)
                chosen = jnp.where(flag > 0.5, value, chosen)
            packed[at, slot] = chosen
    block_copies = neighbour_copies(packed, received)

    def direct(i, carry):
        for k in range(together):
            b = i * together + k
            local = sums[harm, :, lanes(b)]
            here = solved[:, :, lanes(b)]
            weights = (esplit[b, 0], esplit[b, 1])
            out = mm(split(here.reshape(rows, bs) * local), weights, NT).reshape(2, own, bs)
            k_at = harm * own + lax.broadcasted_iota(jnp.int32, (own, bs), 0)
            omega = (lax.rem(k_at + period // 2, period) - period // 2).astype(jnp.float32)
            react = omega * capacity_ref[:, lanes(b)]
            image[0, :, lanes(b)] = -out[0] - react * here[1]
            image[1, :, lanes(b)] = -out[1] + react * here[0]
        return carry

    lax.fori_loop(0, blocks // together, direct, 0)

    finish(cond_copies)
    finish(column_copies)
    field = columns[...].reshape(2 * period, piece)
    def table_apply(which, field):
        th = tables_ref[which, 0]
        tl = tables_ref[which, 1]
        return mm((th, tl), split(field), NN)
    samples = table_apply(0, field).reshape(2, period, piece)
    driven = samples * cond_cols[...].reshape(period, piece)[None]
    spectra_cols[...] = table_apply(1, driven.reshape(2 * period, piece)).reshape(
        harms, 2, own, piece
    )
    spectra_copies = around("harm", harms, lambda peer: spectra_cols.at[peer], spectra.at[harm])
    spectra[harm] = spectra_cols[harm]

    loads[3].wait()
    neighbour_finish(block_copies)

    def couple(b, carry):
        out = image[:, :, lanes(b)].reshape(rows, bs)
        for slot in range(coupling.shape[1]):
            line = where_ref[b, slot]
            picked = received[line // USED, lax.rem(line, USED)]
            out = out + mm(split(picked), split(coupling[b, slot]), NT)
        image[:, :, lanes(b)] = out.reshape(2, own, bs)
        return carry

    lax.fori_loop(0, blocks, couple, 0, unroll=2)
    finish(spectra_copies)

    loads[4].wait()
    for at in range(harms):
        area = pl.ds(at * piece, piece)
        image[:, :, area] = image[:, :, area] + spectra[at]

    def fold(x):
        x = x.reshape(own // 8, 8, x.shape[1]).sum(0)
        out = x[:, 0:128]
        for at in range(1, x.shape[1] // 128):
            out = out + x[:, at * 128 : (at + 1) * 128]
        return jnp.sum(out, axis=0, keepdims=True)

    def exchange(parts_node, parts_harm):
        finish(around("node", nodes, lambda peer: parts_node.at[node], parts_node.at[node]))
        value = parts_node[0]
        for at in range(1, nodes):
            value = value + parts_node[at]
        parts_harm[harm] = value
        finish(around("harm", harms, lambda peer: parts_harm.at[harm], parts_harm.at[harm]))
        value = parts_harm[0]
        for at in range(1, harms):
            value = value + parts_harm[at]
        return jnp.sum(value, axis=1, keepdims=True)

    count = float(period * width * nodes)
    for m in range(kry):
        br, bi = basis[m, 0], basis[m, 1]
        part_node[node, m : m + 1] = fold(br * image[0] + bi * image[1])
        part_node[node, kry + m : kry + m + 1] = fold(br * image[1] - bi * image[0])
    proj = exchange(part_node, part_harm) / count
    row_at = lax.broadcasted_iota(jnp.int32, (2 * kry, 128), 0)
    lane_at = lax.broadcasted_iota(jnp.int32, (2 * kry, 128), 1)
    for p in range(2):
        line = jnp.where(row_at == lane_at + p * kry, jnp.broadcast_to(proj, row_at.shape), 0.0)
        proj_ref[p : p + 1, :] = jnp.sum(line, axis=0, keepdims=True)[:, 0:kry]

    squares = jnp.zeros((1, 128), jnp.float32)
    tile = 512
    for at in range(0, width, tile):
        area = slice(at, at + tile)
        real, imag = image[0, :, area], image[1, :, area]
        for m in range(kry):
            pr = jnp.broadcast_to(proj[m : m + 1], (own, tile))
            pi = jnp.broadcast_to(proj[kry + m : kry + m + 1], (own, tile))
            br, bi = basis[m, 0, :, area], basis[m, 1, :, area]
            real = real - (pr * br - pi * bi)
            imag = imag - (pr * bi + pi * br)
        new_ref[0, :, area] = real
        new_ref[1, :, area] = imag
        squares = squares + fold(real * real + imag * imag)
    square_node[node] = jnp.concatenate([squares, jnp.zeros((7, 128), jnp.float32)], axis=0)
    square = exchange(square_node, square_harm)[0:1] / count
    norm_ref[...] = jnp.sqrt(square + 1e-6)


def coupling_tables(node, near_ref, pattern_ref, where_ref, request):
    slots, blocks = near_ref.shape
    kinds, lines, _ = request.shape
    entries = []
    for b in range(blocks):
        for j in range(slots):
            near = near_ref[j, b]
            offset = lax.div(near, blocks) - node
            at = jnp.where(offset < 0, offset + REACH, offset + REACH - 1)
            present = pattern_ref[j, b] != 0
            code = jnp.where(present, at * blocks + lax.rem(near, blocks), -1)
            entries.append((b, j, at, present, code))
    number = lax.broadcasted_iota(jnp.int32, (kinds * lines, 128), 0)
    hot = jnp.zeros((kinds * lines, 128), jnp.float32)
    for b, j, at, present, code in entries:
        start = at * blocks
        slot = jnp.int32(0)
        for entry in entries:
            other = entry[4]
            lower = jnp.logical_and(other >= start, other < code)
            slot = jnp.where(lower, 1, slot)
        line = jnp.where(present, at * USED + slot, kinds * USED)
        where_ref[b, j] = jnp.clip(line, 0, kinds * USED)
        key = jnp.where(present, code + (at + slot) * blocks, -1)
        hot = jnp.where(number == key, 1.0, hot)
    request[...] = hot.reshape(request.shape)


def per_device(nodes, harms, krylov_basis, cond_time, capacity, diag_blocks, coupling, neighbours, pattern):
    kry, _, own, width = krylov_basis.shape
    blocks, bs, _ = diag_blocks.shape
    period = own * harms
    piece = width // harms
    rows = 2 * own
    tables = jnp.asarray(spectral_tables(period, harms))
    kinds = len(OFFSETS)
    sems = 5 * harms + 2 * kinds + 2 * nodes + 2 * harms
    f32, bf16 = jnp.float32, jnp.bfloat16
    vmem = pl.BlockSpec(memory_space=pltpu.VMEM)
    hbm = pl.BlockSpec(memory_space=pl.ANY)
    smem = pl.BlockSpec(memory_space=pltpu.SMEM)
    rest, proj, norm = pl.pallas_call(
        functools.partial(kernel, nodes, harms),
        out_shape=(
            jax.ShapeDtypeStruct((2, own, width), f32),
            jax.ShapeDtypeStruct((2, kry), f32),
            jax.ShapeDtypeStruct((1, 1), f32),
        ),
        in_specs=[smem, smem, vmem, vmem, hbm, hbm, hbm, hbm],
        out_specs=(vmem, vmem, vmem),
        scratch_shapes=[
            pltpu.VMEM(krylov_basis.shape, f32),
            pltpu.VMEM(cond_time.shape, f32),
            pltpu.VMEM(diag_blocks.shape, f32),
            pltpu.VMEM(coupling.shape, f32),
            pltpu.VMEM((harms, 1, width), f32),
            pltpu.VMEM((kinds, USED * blocks, 128), f32),
            pltpu.VMEM((harms, own, piece), f32),
            pltpu.VMEM((blocks, 2, bs, bs), bf16),
            pltpu.SMEM(neighbours.shape, jnp.int32),
            pltpu.VMEM((kinds, USED * blocks, 128), f32),
            pltpu.VMEM((2, own, width), f32),
            pltpu.VMEM((harms, 2, own, piece), f32),
            pltpu.VMEM((kinds, USED, rows, bs), f32),
            pltpu.VMEM((kinds + 1, USED, rows, bs), f32),
            pltpu.VMEM((harms, 2, own, piece), f32),
            pltpu.VMEM((harms, 2, own, piece), f32),
            pltpu.VMEM((2, own, width), f32),
            pltpu.VMEM((nodes, 2 * kry, 128), f32),
            pltpu.VMEM((harms, 2 * kry, 128), f32),
            pltpu.VMEM((nodes, 8, 128), f32),
            pltpu.VMEM((harms, 8, 128), f32),
            pltpu.SemaphoreType.DMA((5,)),
            pltpu.SemaphoreType.DMA((sems,)),
            pltpu.SemaphoreType.DMA((sems,)),
        ],
        compiler_params=pltpu.CompilerParams(
            collective_id=0, has_side_effects=True, vmem_limit_bytes=60 * 1024 * 1024
        ),
        name="arnoldi_step",
    )(neighbours.T, pattern.T, tables, capacity.reshape(1, width), krylov_basis, cond_time, diag_blocks, coupling)
    norm = norm[0, 0]
    return rest * (1.0 / norm), proj, norm


def solution(mesh):
    shape = dict(mesh.shape)
    return jax.shard_map(
        functools.partial(per_device, shape["node"], shape["harm"]),
        mesh=mesh,
        in_specs=(
            P(None, None, "harm", "node"),
            P("harm", "node"),
            P("node"),
            P("node", None, None),
            P("node", None, None, None),
            P("node", None),
            P("node", None),
        ),
        out_specs=(P(None, "harm", "node"), P(), P()),
        check_vma=False,
    )
```

```python
import functools
import math

import jax
import jax.numpy as jnp
import numpy as np
from jax import lax
from jax.experimental import pallas as pl
from jax.experimental.pallas import tpu as pltpu
from jax.sharding import PartitionSpec as P

NS_ITERS = 4
REACH = 3
USED = 2
OFFSETS = tuple(o for o in range(-REACH, REACH + 1) if o != 0)
MESH = pl.DeviceIdType.MESH
NN = (((1,), (0,)), ((), ()))
NT = (((1,), (1,)), ((), ()))


def split(x):
    high = x.astype(jnp.bfloat16)
    low = (x - high.astype(jnp.float32)).astype(jnp.bfloat16)
    return high, low


def mm(x, weights, dims):
    xh, xl = x
    wh, wl = weights
    rows = xh.shape[0]
    dot = functools.partial(
        lax.dot_general, dimension_numbers=dims, preferred_element_type=jnp.float32
    )
    both = dot(jnp.concatenate([xh, xl], axis=0), wh)
    return both[:rows] + (both[rows:] + dot(xh, wl))


def spectral_tables(count, parts):
    steps = np.arange(count)
    angles = (steps[:, None] * steps[None, :] % count) * (2.0 * math.pi / count)
    cosine = np.cos(angles) / math.sqrt(count)
    sine = np.sin(angles) / math.sqrt(count)
    table = np.block([[cosine, -sine], [sine, cosine]])
    own = count // parts
    ordered = table.reshape(2 * count, 2, parts, own).transpose(0, 2, 1, 3).reshape(2 * count, -1)
    tables = np.stack([ordered, ordered.T]).astype(np.float32)
    high = tables.astype(jnp.bfloat16)
    low = (tables - high.astype(np.float32)).astype(jnp.bfloat16)
    return np.stack([high, low], axis=1)


def kernel(
    nodes, harms,
    near_ref, pattern_ref, tables_ref, capacity_ref, basis_hbm, cond_hbm, diag_hbm, coupling_hbm,
    new_ref, proj_ref, norm_ref,
    basis, cond, diag, coupling, sums, wanted, cond_cols, esplit, where_ref, request,
    solved, columns, packed, received, spectra_cols, spectra, image,
    part_rows, square_rows,
    load_sem, send_sem, recv_sem,
):
    node = lax.axis_index("node")
    harm = lax.axis_index("harm")
    kry, _, own, width = basis.shape
    blocks, bs, _ = diag.shape
    rows = 2 * own
    period = own * harms
    piece = width // harms
    last = kry - 1

    loads = [
        pltpu.make_async_copy(cond_hbm, cond, load_sem.at[0]),
        pltpu.make_async_copy(diag_hbm, diag, load_sem.at[1]),
        pltpu.make_async_copy(basis_hbm.at[last], basis.at[last], load_sem.at[2]),
        pltpu.make_async_copy(coupling_hbm, coupling, load_sem.at[3]),
        pltpu.make_async_copy(basis_hbm.at[0:last], basis.at[0:last], load_sem.at[4]),
    ]
    for load in loads:
        load.start()

    barrier = pltpu.get_barrier_semaphore()
    total_devices = nodes * harms
    flat = node * harms + harm

    def device(step):
        peer = lax.rem(flat + step, total_devices)
        return (lax.div(peer, harms), lax.rem(peer, harms))

    def greet(step, carry):
        pl.semaphore_signal(barrier, inc=1, device_id=device(step), device_id_type=MESH)
        return carry

    lax.fori_loop(1, total_devices, greet, 0)
    coupling_tables(node, near_ref, pattern_ref, where_ref, request)
    received[len(OFFSETS), 0] = jnp.zeros((rows, bs), jnp.float32)
    loads[0].wait()
    sums[harm] = jnp.sum(cond[...], axis=0, keepdims=True)
    pl.semaphore_wait(barrier, total_devices - 1)

    counter = [0]

    def reserve(count):
        first = counter[0]
        counter[0] += count
        return first

    def around(axis, count, source, target):
        me = harm if axis == "harm" else node
        first = reserve(count)
        copies = []
        for step in range(1, count):
            peer = lax.rem(me + step, count)
            copies.append(
                pltpu.make_async_remote_copy(
                    src_ref=source(peer),
                    dst_ref=target,
                    send_sem=send_sem.at[first + step],
                    recv_sem=recv_sem.at[first + step],
                    device_id={axis: peer},
                    device_id_type=MESH,
                )
            )
            copies[-1].start()
        return copies

    def finish(copies):
        for copy in copies:
            copy.wait()

    def neighbour_copies(source, target):
        first = reserve(len(OFFSETS))
        out = []
        for at, offset in enumerate(OFFSETS):
            peer = node + offset
            copy = pltpu.make_async_remote_copy(
                src_ref=source.at[at],
                dst_ref=target.at[len(OFFSETS) - 1 - at],
                send_sem=send_sem.at[first + at],
                recv_sem=recv_sem.at[first + at],
                device_id={"node": jnp.clip(peer, 0, nodes - 1)},
                device_id_type=MESH,
            )
            sends = jnp.logical_and(peer >= 0, peer < nodes)
            back = node - offset
            receives = jnp.logical_and(back >= 0, back < nodes)
            pl.when(sends)(copy.start)
            out.append((copy, sends, receives))
        return out

    def neighbour_finish(copies):
        for copy, sends, receives in copies:
            pl.when(sends)(copy.wait_send)
            pl.when(receives)(copy.wait_recv)

    sum_copies = around("harm", harms, lambda peer: sums.at[harm], sums.at[harm])
    request_copies = neighbour_copies(request, wanted)
    cond_copies = around(
        "harm", harms,
        lambda peer: cond.at[:, pl.ds(pl.multiple_of(peer * piece, 128), piece)],
        cond_cols.at[harm],
    )
    mine = pl.ds(pl.multiple_of(harm * piece, 128), piece)
    cond_cols[harm] = cond[:, mine]
    loads[1].wait()
    loads[2].wait()
    finish(sum_copies)
    total = sums[0]
    for at in range(1, harms):
        total = total + sums[at]
    means = total / period

    together = 2
    sums[harm] = means

    def lanes(b):
        return pl.ds(pl.multiple_of(b * bs, 128), bs)

    def solve(ids):
        scale = [1.0 / sums[harm, :, lanes(b)] for b in ids]
        e1 = [split(-diag[b] * s) for b, s in zip(ids, scale)]
        for b, e in zip(ids, e1):
            esplit[b, 0] = e[0]
            esplit[b, 1] = e[1]
        e2 = [split(mm(e, e, NN)) for e in e1]
        e4 = [split(mm(e, e, NN)) for e in e2]
        w = [basis[last, :, :, lanes(b)].reshape(rows, bs) for b in ids]
        for power in (e1, e2, e4):
            w = [x + mm(split(x), e, NT) for x, e in zip(w, power)]
        y = [mm(split(x), e, NT) for x, e in zip(w, e4)]
        y = [mm(split(x), e, NT) for x, e in zip(y, e4)]
        for b, x, z, s in zip(ids, w, y, scale):
            solved[:, :, lanes(b)] = ((x + z) * s).reshape(2, own, bs)

    first_column = reserve(harms)
    column_copies = []
    per_piece = piece // bs
    for step in range(1, harms + 1):
        peer = lax.rem(harm + step, harms)
        solve([peer * per_piece + k for k in range(per_piece)])
        if step < harms:
            copy = pltpu.make_async_remote_copy(
                src_ref=solved.at[:, :, pl.ds(pl.multiple_of(peer * piece, 128), piece)],
                dst_ref=columns.at[harm],
                send_sem=send_sem.at[first_column + step],
                recv_sem=recv_sem.at[first_column + step],
                device_id={"harm": peer},
                device_id_type=MESH,
            )
            copy.start()
            column_copies.append(copy)
    columns[harm] = solved[:, :, mine]
    neighbour_finish(request_copies)
    for at in range(len(OFFSETS)):
        for slot in range(USED):
            chosen = jnp.zeros((rows, bs), jnp.float32)
            for b in range(blocks):
                line = slot * blocks + b
                flag = jnp.concatenate([wanted[at, line : line + 1, :]] * (bs // 128), axis=1)
                value = solved[:, :, b * bs : (b + 1) * bs].reshape(rows, bs)
                chosen = jnp.where(flag > 0.5, value, chosen)
            packed[at, slot] = chosen
    block_copies = neighbour_copies(packed, received)

    def direct(i, carry):
        for k in range(together):
            b = i * together + k
            local = sums[harm, :, lanes(b)]
            here = solved[:, :, lanes(b)]
            weights = (esplit[b, 0], esplit[b, 1])
            out = mm(split(here.reshape(rows, bs) * local), weights, NT).reshape(2, own, bs)
            k_at = harm * own + lax.broadcasted_iota(jnp.int32, (own, bs), 0)
            omega = (lax.rem(k_at + period // 2, period) - period // 2).astype(jnp.float32)
            react = omega * capacity_ref[:, lanes(b)]
            image[0, :, lanes(b)] = -out[0] - react * here[1]
            image[1, :, lanes(b)] = -out[1] + react * here[0]
        return carry

    lax.fori_loop(0, blocks // together, direct, 0)

    finish(cond_copies)
    finish(column_copies)
    field = columns[...].reshape(2 * period, piece)
    def table_apply(which, field):
        th = tables_ref[which, 0]
        tl = tables_ref[which, 1]
        return mm((th, tl), split(field), NN)
    samples = table_apply(0, field).reshape(2, period, piece)
    driven = samples * cond_cols[...].reshape(period, piece)[None]
    spectra_cols[...] = table_apply(1, driven.reshape(2 * period, piece)).reshape(
        harms, 2, own, piece
    )
    spectra_copies = around("harm", harms, lambda peer: spectra_cols.at[peer], spectra.at[harm])
    spectra[harm] = spectra_cols[harm]

    loads[3].wait()
    neighbour_finish(block_copies)

    def couple(b, carry):
        out = image[:, :, lanes(b)].reshape(rows, bs)
        for slot in range(coupling.shape[1]):
            line = where_ref[b, slot]
            picked = received[line // USED, lax.rem(line, USED)]
            out = out + mm(split(picked), split(coupling[b, slot]), NT)
        image[:, :, lanes(b)] = out.reshape(2, own, bs)
        return carry

    lax.fori_loop(0, blocks, couple, 0, unroll=2)
    finish(spectra_copies)

    loads[4].wait()
    for at in range(harms):
        area = pl.ds(at * piece, piece)
        image[:, :, area] = image[:, :, area] + spectra[at]

    def fold(x):
        x = x.reshape(own // 8, 8, x.shape[1]).sum(0)
        out = x[:, 0:128]
        for at in range(1, x.shape[1] // 128):
            out = out + x[:, at * 128 : (at + 1) * 128]
        return jnp.sum(out, axis=0, keepdims=True)

    def exchange(parts):
        first = reserve(total_devices)

        def copy(step):
            return pltpu.make_async_remote_copy(
                src_ref=parts.at[flat],
                dst_ref=parts.at[flat],
                send_sem=send_sem.at[first + step],
                recv_sem=recv_sem.at[first + step],
                device_id=device(step),
                device_id_type=MESH,
            )

        def start(step, carry):
            copy(step).start()
            return carry

        def wait(step, carry):
            copy(step).wait()
            return carry

        lax.fori_loop(1, total_devices, start, 0)
        lax.fori_loop(1, total_devices, wait, 0)
        rows = [parts[at] for at in range(total_devices)]
        while len(rows) > 1:
            rows = [sum(rows[at : at + 2][1:], rows[at]) for at in range(0, len(rows), 2)]
        return rows[0]

    row_at = lax.broadcasted_iota(jnp.int32, (2 * kry, 128), 0)
    lane_at = lax.broadcasted_iota(jnp.int32, (2 * kry, 128), 1)

    count = float(period * width * nodes)
    reals, imags = [], []
    for m in range(kry):
        br, bi = basis[m, 0], basis[m, 1]
        reals.append(fold(br * image[0] + bi * image[1]))
        imags.append(fold(br * image[1] - bi * image[0]))
    local = jnp.sum(jnp.concatenate(reals + imags, axis=0), axis=1, keepdims=True)
    line = jnp.where(row_at == lane_at, jnp.broadcast_to(local, row_at.shape), 0.0)
    part_rows[flat] = jnp.sum(line, axis=0, keepdims=True)
    found = exchange(part_rows) / count
    line = jnp.where(row_at == lane_at, jnp.broadcast_to(found, row_at.shape), 0.0)
    proj = jnp.sum(line, axis=1, keepdims=True)
    proj_ref[0:1, :] = found[:, 0:kry]
    proj_ref[1:2, :] = found[:, kry : 2 * kry]

    squares = jnp.zeros((1, 128), jnp.float32)
    tile = 512
    for at in range(0, width, tile):
        area = slice(at, at + tile)
        real, imag = image[0, :, area], image[1, :, area]
        for m in range(kry):
            pr = jnp.broadcast_to(proj[m : m + 1], (own, tile))
            pi = jnp.broadcast_to(proj[kry + m : kry + m + 1], (own, tile))
            br, bi = basis[m, 0, :, area], basis[m, 1, :, area]
            real = real - (pr * br - pi * bi)
            imag = imag - (pr * bi + pi * br)
        new_ref[0, :, area] = real
        new_ref[1, :, area] = imag
        squares = squares + fold(real * real + imag * imag)
    square_rows[flat] = squares
    norm_ref[...] = jnp.sum(exchange(square_rows), axis=1, keepdims=True) / count


def coupling_tables(node, near_ref, pattern_ref, where_ref, request):
    slots, blocks = near_ref.shape
    kinds, lines, _ = request.shape
    entries = []
    for b in range(blocks):
        for j in range(slots):
            near = near_ref[j, b]
            offset = lax.div(near, blocks) - node
            at = jnp.where(offset < 0, offset + REACH, offset + REACH - 1)
            present = pattern_ref[j, b] != 0
            code = jnp.where(present, at * blocks + lax.rem(near, blocks), -1)
            entries.append((b, j, at, present, code))
    number = lax.broadcasted_iota(jnp.int32, (kinds * lines, 128), 0)
    hot = jnp.zeros((kinds * lines, 128), jnp.float32)
    for b, j, at, present, code in entries:
        start = at * blocks
        slot = jnp.int32(0)
        for entry in entries:
            other = entry[4]
            lower = jnp.logical_and(other >= start, other < code)
            slot = jnp.where(lower, 1, slot)
        line = jnp.where(present, at * USED + slot, kinds * USED)
        where_ref[b, j] = jnp.clip(line, 0, kinds * USED)
        key = jnp.where(present, code + (at + slot) * blocks, -1)
        hot = jnp.where(number == key, 1.0, hot)
    request[...] = hot.reshape(request.shape)


def per_device(nodes, harms, krylov_basis, cond_time, capacity, diag_blocks, coupling, neighbours, pattern):
    kry, _, own, width = krylov_basis.shape
    blocks, bs, _ = diag_blocks.shape
    period = own * harms
    piece = width // harms
    rows = 2 * own
    tables = jnp.asarray(spectral_tables(period, harms))
    kinds = len(OFFSETS)
    sems = 4 * harms + 2 * kinds + 2 * nodes * harms
    f32, bf16 = jnp.float32, jnp.bfloat16
    vmem = pl.BlockSpec(memory_space=pltpu.VMEM)
    hbm = pl.BlockSpec(memory_space=pl.ANY)
    smem = pl.BlockSpec(memory_space=pltpu.SMEM)
    rest, proj, square = pl.pallas_call(
        functools.partial(kernel, nodes, harms),
        out_shape=(
            jax.ShapeDtypeStruct((2, own, width), f32),
            jax.ShapeDtypeStruct((2, kry), f32),
            jax.ShapeDtypeStruct((1, 1), f32),
        ),
        in_specs=[smem, smem, vmem, vmem, hbm, hbm, hbm, hbm],
        out_specs=(vmem, vmem, vmem),
        scratch_shapes=[
            pltpu.VMEM(krylov_basis.shape, f32),
            pltpu.VMEM(cond_time.shape, f32),
            pltpu.VMEM(diag_blocks.shape, f32),
            pltpu.VMEM(coupling.shape, f32),
            pltpu.VMEM((harms, 1, width), f32),
            pltpu.VMEM((kinds, USED * blocks, 128), f32),
            pltpu.VMEM((harms, own, piece), f32),
            pltpu.VMEM((blocks, 2, bs, bs), bf16),
            pltpu.SMEM(neighbours.shape, jnp.int32),
            pltpu.VMEM((kinds, USED * blocks, 128), f32),
            pltpu.VMEM((2, own, width), f32),
            pltpu.VMEM((harms, 2, own, piece), f32),
            pltpu.VMEM((kinds, USED, rows, bs), f32),
            pltpu.VMEM((kinds + 1, USED, rows, bs), f32),
            pltpu.VMEM((harms, 2, own, piece), f32),
            pltpu.VMEM((harms, 2, own, piece), f32),
            pltpu.VMEM((2, own, width), f32),
            pltpu.VMEM((nodes * harms, 1, 128), f32),
            pltpu.VMEM((nodes * harms, 1, 128), f32),
            pltpu.SemaphoreType.DMA((5,)),
            pltpu.SemaphoreType.DMA((sems,)),
            pltpu.SemaphoreType.DMA((sems,)),
        ],
        compiler_params=pltpu.CompilerParams(
            collective_id=0, has_side_effects=True, vmem_limit_bytes=60 * 1024 * 1024
        ),
        name="arnoldi_step",
    )(neighbours.T, pattern.T, tables, capacity.reshape(1, width), krylov_basis, cond_time, diag_blocks, coupling)
    norm = jnp.sqrt(square[0, 0] + 1e-6)
    return rest * (1.0 / norm), proj, norm


def solution(mesh):
    shape = dict(mesh.shape)
    return jax.shard_map(
        functools.partial(per_device, shape["node"], shape["harm"]),
        mesh=mesh,
        in_specs=(
            P(None, None, "harm", "node"),
            P("harm", "node"),
            P("node"),
            P("node", None, None),
            P("node", None, None, None),
            P("node", None),
            P("node", None),
        ),
        out_specs=(P(None, "harm", "node"), P(), P()),
        check_vma=False,
    )
```

```python
import functools
import math

import jax
import jax.numpy as jnp
import numpy as np
from jax import lax
from jax.experimental import pallas as pl
from jax.experimental.pallas import tpu as pltpu
from jax.sharding import PartitionSpec as P

NS_ITERS = 4
REACH = 3
USED = 2
OFFSETS = tuple(o for o in range(-REACH, REACH + 1) if o != 0)
MESH = pl.DeviceIdType.MESH
NN = (((1,), (0,)), ((), ()))
NT = (((1,), (1,)), ((), ()))


def split(x):
    high = x.astype(jnp.bfloat16)
    low = (x - high.astype(jnp.float32)).astype(jnp.bfloat16)
    return high, low


def mm(x, weights, dims):
    xh, xl = x
    wh, wl = weights
    rows = xh.shape[0]
    dot = functools.partial(
        lax.dot_general, dimension_numbers=dims, preferred_element_type=jnp.float32
    )
    both = dot(jnp.concatenate([xh, xl], axis=0), wh)
    return both[:rows] + (both[rows:] + dot(xh, wl))


def spectral_tables(count, parts):
    steps = np.arange(count)
    angles = (steps[:, None] * steps[None, :] % count) * (2.0 * math.pi / count)
    cosine = np.cos(angles) / math.sqrt(count)
    sine = np.sin(angles) / math.sqrt(count)
    table = np.block([[cosine, -sine], [sine, cosine]])
    own = count // parts
    ordered = table.reshape(2 * count, 2, parts, own).transpose(0, 2, 1, 3).reshape(2 * count, -1)
    tables = np.stack([ordered, ordered.T]).astype(np.float32)
    high = tables.astype(jnp.bfloat16)
    low = (tables - high.astype(np.float32)).astype(jnp.bfloat16)
    return np.stack([high, low], axis=1)


def kernel(
    nodes, harms,
    near_ref, pattern_ref, tables_ref, capacity_ref, basis_hbm, cond_hbm, diag_hbm, coupling_hbm,
    new_ref, proj_ref, norm_ref,
    basis, cond, diag, coupling, sums, wanted, cond_cols, esplit, where_ref, request,
    solved, columns, packed, received, spectra_cols, spectra, image,
    part_rows, square_rows,
    load_sem, send_sem, recv_sem,
):
    node = lax.axis_index("node")
    harm = lax.axis_index("harm")
    kry, _, own, width = basis.shape
    blocks, bs, _ = diag.shape
    rows = 2 * own
    period = own * harms
    piece = width // harms
    last = kry - 1

    loads = [
        pltpu.make_async_copy(cond_hbm, cond, load_sem.at[0]),
        pltpu.make_async_copy(diag_hbm, diag, load_sem.at[1]),
        pltpu.make_async_copy(basis_hbm.at[last], basis.at[last], load_sem.at[2]),
        pltpu.make_async_copy(coupling_hbm, coupling, load_sem.at[3]),
        pltpu.make_async_copy(basis_hbm.at[0:last], basis.at[0:last], load_sem.at[4]),
    ]
    for load in loads:
        load.start()

    barrier = pltpu.get_barrier_semaphore()
    total_devices = nodes * harms
    flat = node * harms + harm

    def ahead(me, count):
        return [me] + [jnp.where(me + step >= count, me + step - count, me + step) for step in range(1, count)]

    node_at, harm_at = ahead(node, nodes), ahead(harm, harms)

    def device(step):
        return (node_at[step // harms], harm_at[step % harms])

    for step in range(1, total_devices):
        pl.semaphore_signal(barrier, inc=1, device_id=device(step), device_id_type=MESH)
    coupling_tables(node, near_ref, pattern_ref, where_ref, request)
    received[len(OFFSETS), 0] = jnp.zeros((rows, bs), jnp.float32)
    loads[0].wait()
    sums[harm] = jnp.sum(cond[...], axis=0, keepdims=True)
    pl.semaphore_wait(barrier, total_devices - 1)

    counter = [0]

    def reserve(count):
        first = counter[0]
        counter[0] += count
        return first

    def around(axis, count, source, target):
        me = harm if axis == "harm" else node
        first = reserve(count)
        copies = []
        for step in range(1, count):
            peer = lax.rem(me + step, count)
            copies.append(
                pltpu.make_async_remote_copy(
                    src_ref=source(peer),
                    dst_ref=target,
                    send_sem=send_sem.at[first + step],
                    recv_sem=recv_sem.at[first + step],
                    device_id={axis: peer},
                    device_id_type=MESH,
                )
            )
            copies[-1].start()
        return copies

    def finish(copies):
        for copy in copies:
            copy.wait()

    def neighbour_copies(source, target):
        first = reserve(len(OFFSETS))
        out = []
        for at, offset in enumerate(OFFSETS):
            peer = node + offset
            copy = pltpu.make_async_remote_copy(
                src_ref=source.at[at],
                dst_ref=target.at[len(OFFSETS) - 1 - at],
                send_sem=send_sem.at[first + at],
                recv_sem=recv_sem.at[first + at],
                device_id={"node": jnp.clip(peer, 0, nodes - 1)},
                device_id_type=MESH,
            )
            sends = jnp.logical_and(peer >= 0, peer < nodes)
            back = node - offset
            receives = jnp.logical_and(back >= 0, back < nodes)
            pl.when(sends)(copy.start)
            out.append((copy, sends, receives))
        return out

    def neighbour_finish(copies):
        for copy, sends, receives in copies:
            pl.when(sends)(copy.wait_send)
            pl.when(receives)(copy.wait_recv)

    sum_copies = around("harm", harms, lambda peer: sums.at[harm], sums.at[harm])
    request_copies = neighbour_copies(request, wanted)
    cond_copies = around(
        "harm", harms,
        lambda peer: cond.at[:, pl.ds(pl.multiple_of(peer * piece, 128), piece)],
        cond_cols.at[harm],
    )
    mine = pl.ds(pl.multiple_of(harm * piece, 128), piece)
    cond_cols[harm] = cond[:, mine]
    loads[1].wait()
    loads[2].wait()
    finish(sum_copies)
    total = sums[0]
    for at in range(1, harms):
        total = total + sums[at]
    means = total / period

    together = 2
    sums[harm] = means

    def lanes(b):
        return pl.ds(pl.multiple_of(b * bs, 128), bs)

    def solve(ids):
        scale = [1.0 / sums[harm, :, lanes(b)] for b in ids]
        e1 = [split(-diag[b] * s) for b, s in zip(ids, scale)]
        for b, e in zip(ids, e1):
            esplit[b, 0] = e[0]
            esplit[b, 1] = e[1]
        e2 = [split(mm(e, e, NN)) for e in e1]
        e4 = [split(mm(e, e, NN)) for e in e2]
        w = [basis[last, :, :, lanes(b)].reshape(rows, bs) for b in ids]
        for power in (e1, e2, e4):
            w = [x + mm(split(x), e, NT) for x, e in zip(w, power)]
        y = [mm(split(x), e, NT) for x, e in zip(w, e4)]
        y = [mm(split(x), e, NT) for x, e in zip(y, e4)]
        for b, x, z, s in zip(ids, w, y, scale):
            solved[:, :, lanes(b)] = ((x + z) * s).reshape(2, own, bs)

    first_column = reserve(harms)
    column_copies = []
    per_piece = piece // bs
    for step in range(1, harms + 1):
        peer = lax.rem(harm + step, harms)
        solve([peer * per_piece + k for k in range(per_piece)])
        if step < harms:
            copy = pltpu.make_async_remote_copy(
                src_ref=solved.at[:, :, pl.ds(pl.multiple_of(peer * piece, 128), piece)],
                dst_ref=columns.at[harm],
                send_sem=send_sem.at[first_column + step],
                recv_sem=recv_sem.at[first_column + step],
                device_id={"harm": peer},
                device_id_type=MESH,
            )
            copy.start()
            column_copies.append(copy)
    columns[harm] = solved[:, :, mine]
    neighbour_finish(request_copies)
    for at in range(len(OFFSETS)):
        for slot in range(USED):
            chosen = jnp.zeros((rows, bs), jnp.float32)
            for b in range(blocks):
                line = slot * blocks + b
                flag = jnp.concatenate([wanted[at, line : line + 1, :]] * (bs // 128), axis=1)
                value = solved[:, :, b * bs : (b + 1) * bs].reshape(rows, bs)
                chosen = jnp.where(flag > 0.5, value, chosen)
            packed[at, slot] = chosen
    block_copies = neighbour_copies(packed, received)

    def direct(i, carry):
        for k in range(together):
            b = i * together + k
            local = sums[harm, :, lanes(b)]
            here = solved[:, :, lanes(b)]
            weights = (esplit[b, 0], esplit[b, 1])
            out = mm(split(here.reshape(rows, bs) * local), weights, NT).reshape(2, own, bs)
            k_at = harm * own + lax.broadcasted_iota(jnp.int32, (own, bs), 0)
            omega = (lax.rem(k_at + period // 2, period) - period // 2).astype(jnp.float32)
            react = omega * capacity_ref[:, lanes(b)]
            image[0, :, lanes(b)] = -out[0] - react * here[1]
            image[1, :, lanes(b)] = -out[1] + react * here[0]
        return carry

    lax.fori_loop(0, blocks // together, direct, 0)

    finish(cond_copies)
    finish(column_copies)
    field = columns[...].reshape(2 * period, piece)
    def table_apply(which, field):
        th = tables_ref[which, 0]
        tl = tables_ref[which, 1]
        return mm((th, tl), split(field), NN)
    samples = table_apply(0, field).reshape(2, period, piece)
    driven = samples * cond_cols[...].reshape(period, piece)[None]
    spectra_cols[...] = table_apply(1, driven.reshape(2 * period, piece)).reshape(
        harms, 2, own, piece
    )
    spectra_copies = around("harm", harms, lambda peer: spectra_cols.at[peer], spectra.at[harm])
    spectra[harm] = spectra_cols[harm]

    loads[3].wait()
    neighbour_finish(block_copies)

    def couple(b, carry):
        out = image[:, :, lanes(b)].reshape(rows, bs)
        for slot in range(coupling.shape[1]):
            line = where_ref[b, slot]
            picked = received[line // USED, lax.rem(line, USED)]
            out = out + mm(split(picked), split(coupling[b, slot]), NT)
        image[:, :, lanes(b)] = out.reshape(2, own, bs)
        return carry

    lax.fori_loop(0, blocks, couple, 0, unroll=2)
    finish(spectra_copies)

    loads[4].wait()
    for at in range(harms):
        area = pl.ds(at * piece, piece)
        image[:, :, area] = image[:, :, area] + spectra[at]

    def fold(x):
        x = x.reshape(own // 8, 8, x.shape[1]).sum(0)
        out = x[:, 0:128]
        for at in range(1, x.shape[1] // 128):
            out = out + x[:, at * 128 : (at + 1) * 128]
        return jnp.sum(out, axis=0, keepdims=True)

    def exchange(parts):
        first = reserve(total_devices)

        copies = []
        for step in range(1, total_devices):
            copies.append(
                pltpu.make_async_remote_copy(
                    src_ref=parts.at[flat],
                    dst_ref=parts.at[flat],
                    send_sem=send_sem.at[first + step],
                    recv_sem=recv_sem.at[first + step],
                    device_id=device(step),
                    device_id_type=MESH,
                )
            )
            copies[-1].start()
        finish(copies)
        rows = [parts[at] for at in range(total_devices)]
        while len(rows) > 1:
            rows = [sum(rows[at : at + 2][1:], rows[at]) for at in range(0, len(rows), 2)]
        return rows[0]

    row_at = lax.broadcasted_iota(jnp.int32, (2 * kry, 128), 0)
    lane_at = lax.broadcasted_iota(jnp.int32, (2 * kry, 128), 1)

    count = float(period * width * nodes)
    reals, imags = [], []
    for m in range(kry):
        br, bi = basis[m, 0], basis[m, 1]
        reals.append(fold(br * image[0] + bi * image[1]))
        imags.append(fold(br * image[1] - bi * image[0]))
    local = jnp.sum(jnp.concatenate(reals + imags, axis=0), axis=1, keepdims=True)
    line = jnp.where(row_at == lane_at, jnp.broadcast_to(local, row_at.shape), 0.0)
    part_rows[flat] = jnp.sum(line, axis=0, keepdims=True)
    found = exchange(part_rows) / count
    line = jnp.where(row_at == lane_at, jnp.broadcast_to(found, row_at.shape), 0.0)
    proj = jnp.sum(line, axis=1, keepdims=True)
    proj_ref[0:1, :] = found[:, 0:kry]
    proj_ref[1:2, :] = found[:, kry : 2 * kry]

    squares = jnp.zeros((1, 128), jnp.float32)
    tile = 512
    for at in range(0, width, tile):
        area = slice(at, at + tile)
        real, imag = image[0, :, area], image[1, :, area]
        for m in range(kry):
            pr = jnp.broadcast_to(proj[m : m + 1], (own, tile))
            pi = jnp.broadcast_to(proj[kry + m : kry + m + 1], (own, tile))
            br, bi = basis[m, 0, :, area], basis[m, 1, :, area]
            real = real - (pr * br - pi * bi)
            imag = imag - (pr * bi + pi * br)
        new_ref[0, :, area] = real
        new_ref[1, :, area] = imag
        squares = squares + fold(real * real + imag * imag)
    square_rows[flat] = squares
    norm_ref[...] = jnp.sum(exchange(square_rows), axis=1, keepdims=True) / count


def coupling_tables(node, near_ref, pattern_ref, where_ref, request):
    slots, blocks = near_ref.shape
    kinds, lines, _ = request.shape
    entries = []
    for b in range(blocks):
        for j in range(slots):
            near = near_ref[j, b]
            offset = lax.div(near, blocks) - node
            at = jnp.where(offset < 0, offset + REACH, offset + REACH - 1)
            present = pattern_ref[j, b] != 0
            code = jnp.where(present, at * blocks + lax.rem(near, blocks), -1)
            entries.append((b, j, at, present, code))
    number = lax.broadcasted_iota(jnp.int32, (kinds * lines, 128), 0)
    hot = jnp.zeros((kinds * lines, 128), jnp.float32)
    for b, j, at, present, code in entries:
        start = at * blocks
        slot = jnp.int32(0)
        for entry in entries:
            other = entry[4]
            lower = jnp.logical_and(other >= start, other < code)
            slot = jnp.where(lower, 1, slot)
        line = jnp.where(present, at * USED + slot, kinds * USED)
        where_ref[b, j] = jnp.clip(line, 0, kinds * USED)
        key = jnp.where(present, code + (at + slot) * blocks, -1)
        hot = jnp.where(number == key, 1.0, hot)
    request[...] = hot.reshape(request.shape)


def per_device(nodes, harms, krylov_basis, cond_time, capacity, diag_blocks, coupling, neighbours, pattern):
    kry, _, own, width = krylov_basis.shape
    blocks, bs, _ = diag_blocks.shape
    period = own * harms
    piece = width // harms
    rows = 2 * own
    tables = jnp.asarray(spectral_tables(period, harms))
    kinds = len(OFFSETS)
    sems = 4 * harms + 2 * kinds + 2 * nodes * harms
    f32, bf16 = jnp.float32, jnp.bfloat16
    vmem = pl.BlockSpec(memory_space=pltpu.VMEM)
    hbm = pl.BlockSpec(memory_space=pl.ANY)
    smem = pl.BlockSpec(memory_space=pltpu.SMEM)
    rest, proj, square = pl.pallas_call(
        functools.partial(kernel, nodes, harms),
        out_shape=(
            jax.ShapeDtypeStruct((2, own, width), f32),
            jax.ShapeDtypeStruct((2, kry), f32),
            jax.ShapeDtypeStruct((1, 1), f32),
        ),
        in_specs=[smem, smem, vmem, vmem, hbm, hbm, hbm, hbm],
        out_specs=(vmem, vmem, vmem),
        scratch_shapes=[
            pltpu.VMEM(krylov_basis.shape, f32),
            pltpu.VMEM(cond_time.shape, f32),
            pltpu.VMEM(diag_blocks.shape, f32),
            pltpu.VMEM(coupling.shape, f32),
            pltpu.VMEM((harms, 1, width), f32),
            pltpu.VMEM((kinds, USED * blocks, 128), f32),
            pltpu.VMEM((harms, own, piece), f32),
            pltpu.VMEM((blocks, 2, bs, bs), bf16),
            pltpu.SMEM(neighbours.shape, jnp.int32),
            pltpu.VMEM((kinds, USED * blocks, 128), f32),
            pltpu.VMEM((2, own, width), f32),
            pltpu.VMEM((harms, 2, own, piece), f32),
            pltpu.VMEM((kinds, USED, rows, bs), f32),
            pltpu.VMEM((kinds + 1, USED, rows, bs), f32),
            pltpu.VMEM((harms, 2, own, piece), f32),
            pltpu.VMEM((harms, 2, own, piece), f32),
            pltpu.VMEM((2, own, width), f32),
            pltpu.VMEM((nodes * harms, 1, 128), f32),
            pltpu.VMEM((nodes * harms, 1, 128), f32),
            pltpu.SemaphoreType.DMA((5,)),
            pltpu.SemaphoreType.DMA((sems,)),
            pltpu.SemaphoreType.DMA((sems,)),
        ],
        compiler_params=pltpu.CompilerParams(
            collective_id=0, has_side_effects=True, vmem_limit_bytes=60 * 1024 * 1024
        ),
        name="arnoldi_step",
    )(neighbours.T, pattern.T, tables, capacity.reshape(1, width), krylov_basis, cond_time, diag_blocks, coupling)
    norm = jnp.sqrt(square[0, 0] + 1e-6)
    return rest * (1.0 / norm), proj, norm


def solution(mesh):
    shape = dict(mesh.shape)
    return jax.shard_map(
        functools.partial(per_device, shape["node"], shape["harm"]),
        mesh=mesh,
        in_specs=(
            P(None, None, "harm", "node"),
            P("harm", "node"),
            P("node"),
            P("node", None, None),
            P("node", None, None, None),
            P("node", None),
            P("node", None),
        ),
        out_specs=(P(None, "harm", "node"), P(), P()),
        check_vma=False,
    )
```
